32 devices in a mesh: dp: 8 (over y, x, core), own: 4 (over z).
Axes of the slice: x: 2, y: 2, z: 4, core: 2. Of those that a mesh axis runs over, the one named last changes fastest.
Arguments:
- grads: bfloat16 [8, 6, 8192, 128], P('dp', None, 'own'), may hold values from -6 to 6
- proj: bfloat16 [4, 3, 8192, 1024], P('own', None, 'dp'), may hold values from -0.0625 to 0.0625
- moment1: float32 [4, 3, 1024, 128], P('own', None, 'dp'), may hold values from -24 to 24
- moment2: float32 [4, 3, 1024, 128], P('own', None, 'dp'), may hold values from 0.05 to 5
- plan: int32 [6], replicated, may hold values from 0 to 3, as said below
Outputs:
- update: bfloat16 [6, 8192, 128], P(None, 'own')
- new_moment1: float32 [4, 3, 1024, 128], P('own', None, 'dp')
- new_moment2: float32 [4, 3, 1024, 128], P('own', None, 'dp')
The draws below stay inside these ranges and needn't reach their ends.
Inputs may be any that keep to these rules, and one draw needn't show every extreme that they name: `plan`: no owner is named more than 3 times, and some owner is named exactly 3 times.
All inputs are finite; a program needn't handle non-finite values.
Results may differ from the reference program's by a relative error of at most 0.015.
Values may be sent and summed in bfloat16 or wider, within the bound.
A program may use at most 64 MiB of HBM per device.

```python
import math
import jax
import jax.numpy as jnp
from jax import lax

D = 8192
RANK = 1024
COLS = 128
CAP = 3
MATS = 6
N_DP = 8
N_OWN = 4


def draw_plan(key, part):
    places = N_OWN * CAP
    key_score, key_full, key_order = jax.random.split(key, 3)
    scores = jax.random.randint(key_score, (places,), 0, 1000)
    favored = jax.random.randint(key_full, (), 0, N_OWN)
    owners = jnp.arange(places, dtype=jnp.int32) // CAP
    ranked = scores * places + jnp.arange(places, dtype=jnp.int32) + jnp.where(owners == favored, 1000 * places, 0)
    chosen = jnp.argsort(-ranked, stable=True)[:MATS]
    picked = owners[chosen]
    shuffle = jax.random.permutation(key_order, MATS)
    return picked[shuffle].astype(jnp.int32)


def block_levels(stream_key, extent, pieces, low, high):
    def one(axis_at, blocks):
        heights = jax.random.uniform(jax.random.fold_in(jax.random.fold_in(stream_key, 6), axis_at), (blocks,), jnp.float32, low / len(pieces), high / len(pieces))
        return jnp.repeat(jnp.exp(heights), extent[axis_at] // blocks).reshape((-1,) + (1,) * (len(extent) - axis_at - 1))

    level = one(*pieces[0])
    for cut in pieces[1:]:
        level = level * one(*cut)
    return level


def scatter_about(stream_key, dims, scale, limit, pieces=(), kind=jnp.bfloat16):
    array = jax.random.normal(stream_key, dims, jnp.float32) * scale
    if len(pieces) > 0:
        array = block_levels(stream_key, dims, pieces, -0.22, 0.18) * array
    return jnp.clip(array, min=-limit, max=limit).astype(kind)


def setup_inputs(seed: int = 0) -> dict:
    key_list = jax.random.split(jax.random.key(seed), 6)
    return {
        "grads": scatter_about(key_list[0], (N_DP, MATS, D, COLS), 1.0, 6.0, ((0, 8), (2, 4))),
        "proj": scatter_about(key_list[1], (N_OWN, CAP, D, RANK), D ** -0.5, 0.0625, ((0, 4), (2, 8))),
        "moment1": scatter_about(key_list[2], (N_OWN, CAP, RANK, COLS), 4.0, 24.0, ((0, 4), (2, 8)), jnp.float32),
        "moment2": jnp.clip(jnp.exp(math.log(5.0) - 4.6051702 * jax.random.uniform(key_list[3], (N_OWN, CAP, RANK, COLS), jnp.float32) ** block_levels(key_list[3], (N_OWN, CAP, RANK, COLS), ((0, 4), (2, 8)), -0.2, 0.2)), 0.05, 5.0),
        "plan": draw_plan(jax.random.fold_in(key_list[5], 71), 0),
    }


beta_one = 0.9
beta_two = 0.999
adam_eps = 1e-08
norm_eps = 1e-06
correct_one = 1.0 - 0.9 ** 10
correct_two = 1.0 - 0.999 ** 10

def slot_selector(plan):
    matrices = plan.shape[0]
    places = jnp.arange(N_OWN * CAP, dtype=jnp.int32)
    owners = places // CAP
    within = places % CAP
    index = jnp.arange(matrices, dtype=jnp.int32)
    before = lax.optimization_barrier(jnp.sum(((plan[None, :] == plan[:, None]) & (index[None, :] < index[:, None])).astype(jnp.int32), axis=1))
    chosen = (plan[None, :] == owners[:, None]) & (before[None, :] == within[:, None])
    return chosen.astype(jnp.float32)

def reference(grads, proj, moment1, moment2, plan):
    selector = slot_selector(plan)
    total = lax.optimization_barrier(jnp.sum(grads.astype(jnp.float32), axis=0))
    slot_grad = jnp.einsum('sj,jdc->sdc', selector, total)
    grad_half = lax.optimization_barrier(slot_grad.astype(jnp.bfloat16))
    projection = proj.reshape(N_OWN * CAP, D, RANK).astype(jnp.float32)
    rank_grad = jnp.einsum('sdr,sdc->src', projection, grad_half.astype(jnp.float32))
    first_old = moment1.reshape(N_OWN * CAP, RANK, COLS)
    second_old = moment2.reshape(N_OWN * CAP, RANK, COLS)
    first_new = beta_one * first_old + (1.0 - beta_one) * rank_grad
    second_new = beta_two * second_old + (1.0 - beta_two) * rank_grad * rank_grad
    adam_step = first_new / correct_one / (jnp.sqrt(second_new / correct_two) + adam_eps)
    adam_half = lax.optimization_barrier(adam_step.astype(jnp.bfloat16)).astype(jnp.float32)
    rank_half = lax.optimization_barrier(rank_grad.astype(jnp.bfloat16)).astype(jnp.float32)
    grad_norms = lax.optimization_barrier(jnp.sum(rank_grad * rank_grad, axis=1))
    step_norms = lax.optimization_barrier(jnp.sum(adam_half * adam_half, axis=1))
    column_scale = jnp.sqrt(step_norms) / (jnp.sqrt(grad_norms) + norm_eps)
    combined = lax.optimization_barrier((adam_half - column_scale[:, None, :] * rank_half).astype(jnp.bfloat16))
    slot_update = jnp.einsum('sdr,src->sdc', projection, combined.astype(jnp.float32)) + column_scale[:, None, :] * slot_grad
    update_half = lax.optimization_barrier(slot_update.astype(jnp.bfloat16))
    update = jnp.einsum('sj,sdc->jdc', selector, update_half.astype(jnp.float32)).astype(jnp.bfloat16)
    return (update, first_new.reshape(N_OWN, CAP, RANK, COLS), second_new.reshape(N_OWN, CAP, RANK, COLS))
```

```python
import functools
import jax
import jax.numpy as jnp
from jax import lax
from jax.experimental import pallas as pl
from jax.experimental.pallas import tpu as pltpu
from jax.sharding import PartitionSpec as P

beta_one = 0.9
beta_two = 0.999
adam_eps = 1e-08
norm_eps = 1e-06
correct_one = 1.0 - 0.9**10
correct_two = 1.0 - 0.999**10

CH = 4
CB = 4
F32 = jnp.float32
BF16 = jnp.bfloat16


def rank_ranges(mats, m, cap):
    lo, hi = [mats] * cap, [0] * cap

    def walk(counts, left):
        if len(counts) == cap:
            if left == 0 and counts[-1] >= 1:
                at = 0
                for k, c in enumerate(counts):
                    lo[k] = min(lo[k], at)
                    at += c
                    hi[k] = max(hi[k], at)
            return
        for c in range(min(left, counts[-1] if counts else m), -1, -1):
            walk(counts + [c], left - c)

    walk([], mats)
    return lo, hi


def groups_of(mats, m, cap):
    lo, hi = rank_ranges(mats, m, cap)
    ranks = [[k for k in range(cap) if lo[k] <= q < hi[k]] for q in range(mats)]
    scatter = [(0, hi[0], [k for k in range(cap) if hi[k] <= hi[0]])]
    if hi[0] < mats:
        scatter.append((hi[0], mats, [k for k in range(cap) if hi[k] > hi[0]]))
    gather = []
    for k in range(cap):
        qs = [q for q in range(mats) if max(ranks[q]) == k]
        if qs:
            gather.append((qs[0], qs[-1] + 1, k))
    return ranks, scatter, gather


def plan_scalars(plan, mats):
    owner = [plan[j] for j in range(mats)]
    rank = []
    for j in range(mats):
        before = jnp.int32(0)
        for i in range(j):
            before = before + jnp.where(owner[i] == owner[j], 1, 0)
        rank.append(before)
    key = [rank[j] * mats + j for j in range(mats)]
    pos = []
    for j in range(mats):
        before = jnp.int32(0)
        for i in range(mats):
            if i != j:
                before = before + jnp.where(key[i] < key[j], 1, 0)
        pos.append(before)
    return owner, rank, pos


def kernel(n, m, plan, grads, proj, m1, m2, gat, m1_out, m2_out, sc):
    mats, chips, piece, cols = grads.shape[0], n // 2, grads.shape[3], grads.shape[4]
    cap, rank_rows = m1.shape[0], m1.shape[1]
    rank = n * rank_rows
    wide = 2
    deep = chips // wide
    ranks, scatter, gather = groups_of(mats, m, cap)
    dp = lax.axis_index("dp")
    own = lax.axis_index("own")
    core = lax.rem(dp, 2)
    chip = lax.div(dp, 2)
    xa = lax.rem(chip, wide)
    yb = lax.div(chip, wide)
    other = 1 - core
    partner = (2 * chip + other, own)
    step_f = piece // CH
    step_b = piece // CB

    def at_chip(which):
        return (2 * which + core, own)

    def remote(src, dst, send, recv, device):
        return pltpu.make_async_remote_copy(
            src_ref=src, dst_ref=dst, send_sem=send, recv_sem=recv,
            device_id=device, device_id_type=pl.DeviceIdType.MESH,
        )

    def taken(block, recv):
        remote(block, block, sc["s_pair"].at[0], recv, partner).wait_recv()

    def sent(block, send):
        remote(block, block, send, sc["r_pair"].at[0], partner).wait_send()

    def peers(axis):
        if axis == 0:
            return [(1, 1 - xa, at_chip(wide * yb + 1 - xa))]
        out = []
        for d in range(1, deep):
            y = lax.rem(yb + d, deep)
            out.append((d, y, at_chip(wide * y + xa)))
        return out

    def rows(ch):
        return pl.ds(ch * step_f, step_f)

    def rows_b(ch):
        return pl.ds(ch * step_b, step_b)

    loads = []
    for ch in range(CH):
        c = pltpu.make_async_copy(grads.at[:, core, :, rows(ch)], sc["own_half"][ch], sc["l_own"].at[ch])
        c.start()
        loads.append(c)
    load_proj = pltpu.make_async_copy(proj, sc["weights"], sc["l_rest"].at[0])
    load_proj.start()
    load_m1 = pltpu.make_async_copy(m1, sc["m1"], sc["l_rest"].at[1])
    load_m1.start()
    load_m2 = pltpu.make_async_copy(m2, sc["m2"], sc["l_rest"].at[2])
    load_m2.start()

    barrier = pltpu.get_barrier_semaphore()
    everyone = [(lax.rem(dp + d, n), own) for d in range(1, n)]
    everyone += [(dp, lax.rem(own + dz, m)) for dz in range(1, m)]
    for device in everyone:
        pl.semaphore_signal(barrier, inc=1, device_id=device, device_id_type=pl.DeviceIdType.MESH)
    for d in range(chips):

        @pl.when(jnp.logical_and(chip != own, d != chip))
        def _():
            pl.semaphore_signal(barrier, inc=1, device_id=(2 * d + core, chip), device_id_type=pl.DeviceIdType.MESH)

    owner, rank_of, pos = plan_scalars(plan, mats)
    order, owner_at, rank_at = [], [], []
    for q in range(mats):
        index = jnp.int32(0)
        who = jnp.int32(0)
        which = jnp.int32(0)
        for j in range(mats):
            here = pos[j] == q
            index = jnp.where(here, j, index)
            who = jnp.where(here, owner[j], who)
            which = jnp.where(here, rank_of[j], which)
        order.append(index)
        owner_at.append(who)
        rank_at.append(which)

    slots = {}
    for dz in range(m):
        to = lax.rem(own + dz, m)
        for k in range(cap):
            index = jnp.int32(0)
            valid = jnp.int32(0)
            for j in range(mats):
                here = jnp.logical_and(owner[j] == to, rank_of[j] == k)
                index = jnp.where(here, pos[j], index)
                valid = jnp.where(here, 1, valid)
            slots[dz, k] = (index, valid.astype(F32))

    pl.semaphore_wait(barrier, n - 1 + m - 1 + jnp.where(chip != own, m - 1, 0))

    sends = []

    pair = []
    for ch in range(CH):
        c = remote(
            grads.at[:, other, :, rows(ch)], sc["pair_half"][ch], sc["s_pair"].at[0], sc["r_pair"].at[ch], partner
        )
        c.start()
        pair.append(c)

    live = {}

    def first_sum(g, ch):
        q0, q1, _ = scatter[g]
        if g == 0:
            pair[ch].wait_recv()
            loads[ch].wait()
        hs = sc["hs"][g][ch]
        for q in range(q0, q1):
            value = sc["own_half"][ch][order[q]].astype(F32) + sc["pair_half"][ch][order[q]].astype(F32)
            value = value.astype(BF16)
            for t in range(chips):
                hs[t // wide, t % wide, q - q0] = value[t]
        axis = ch % 2
        out = []
        for d, index, device in peers(axis):
            c = remote(
                hs.at[:, index] if axis == 0 else hs.at[index], sc["r1"][g][ch].at[d - 1],
                sc["s_rs1"].at[g, ch, d - 1], sc["r_rs1"].at[g, ch, d - 1], device,
            )
            c.start()
            out.append(c)
        live["rs1", g, ch] = out

    def second_sum(g, ch):
        axis = ch % 2
        out = live["rs1", g, ch]
        for c in out:
            c.wait_recv()
        hs, r1, s1 = sc["hs"][g][ch], sc["r1"][g][ch], sc["s1"][g][ch]
        for i in range(deep if axis == 0 else wide):
            value = (hs[i, xa] if axis == 0 else hs[yb, i]).astype(F32)
            for c in range(len(out)):
                value = value + r1[c, i].astype(F32)
            s1[i] = value.astype(BF16)
        nxt = []
        for d, index, device in peers(1 - axis):
            c = remote(
                s1.at[index], sc["r2"][g][ch].at[d - 1], sc["s_rs2"].at[g, ch, d - 1], sc["r_rs2"].at[g, ch, d - 1], device
            )
            c.start()
            nxt.append(c)
        live["rs2", g, ch] = nxt
        sends.extend(out + nxt)

    def third_sum(g, ch):
        q0, q1, ready = scatter[g]
        axis = ch % 2
        out = live["rs2", g, ch]
        for c in out:
            c.wait_recv()
        s1, r2, total = sc["s1"][g][ch], sc["r2"][g][ch], sc["total"][ch]
        mine = yb if axis == 0 else xa
        value = s1[mine].astype(F32)
        for c in range(len(out)):
            value = value + r2[c].astype(F32)
        total[q0:q1] = value.astype(BF16)
        ship(ready[0], ch)
        if ch == CH - 1:
            for k in ready[1:]:
                for c in range(CH):
                    ship(k, c)

    def ship(k, ch):
        grad, slot_out = sc["grad"], sc["slot_out"]
        for dz in list(range(1, m)) + [0]:
            to = lax.rem(own + dz, m)
            index, valid = slots[dz, k]
            slot_out[k, ch, dz] = (sc["total"][ch][index].astype(F32) * valid).astype(BF16)
            c = remote(
                slot_out.at[k, ch, dz], grad.at[k, chip, rows(ch)],
                sc["s_slot"].at[1 if dz else 0], sc["r_slot"].at[k, chip], (2 * own + core, to),
            )
            if dz == 0:

                @pl.when(chip != own)
                def _():
                    c.start()

                @pl.when(chip == own)
                def _():
                    grad[k, chip, rows(ch)] = slot_out[k, ch, 0]

            else:
                c.start()

    def project(k):
        grad = sc["grad"]
        for d in range(chips):

            @pl.when(jnp.logical_or(d != chip, chip != own))
            def _():
                taken(grad.at[k, d], sc["r_slot"].at[k, d])

        if k == 0:
            load_proj.wait()
        g = grad[k].reshape(chips * piece, cols)
        w = sc["weights"][k].reshape(chips * piece, rank)
        value = lax.dot_general(g, w, (((0,), (0,)), ((), ())), preferred_element_type=F32)
        value = value.T.astype(BF16)
        part = sc["part"]
        for t in range(chips):
            for s in range(2):
                at = (2 * t + s) * rank_rows
                part[s, k, t] = value[at : at + rank_rows]
        c = remote(part.at[other, k], sc["part_in"].at[k], sc["s_part"].at[k], sc["r_part"].at[k], partner)
        c.start()
        sends.append(c)
        live["part", k] = c

    def share(k):
        live["part", k].wait_recv()
        part, part_in, pair_sum = sc["part"], sc["part_in"], sc["pair_sum"]
        for t in range(chips):
            pair_sum[k, t] = (part[core, k, t].astype(F32) + part_in[k, t].astype(F32)).astype(BF16)
        for d in range(1, chips):
            to = lax.rem(chip + d, chips)
            c = remote(
                pair_sum.at[k, to], sc["share_in"].at[k, d - 1],
                sc["s_share"].at[k], sc["r_share"].at[k], at_chip(to),
            )
            c.start()

    def adam(k):
        taken(sc["share_in"].at[k], sc["r_share"].at[k])
        if k == 0:
            load_m1.wait()
            load_m2.wait()
        value = sc["pair_sum"][k, chip].astype(F32)
        for d in range(1, chips):
            value = value + sc["share_in"][k, d - 1].astype(F32)
        first = beta_one * sc["m1"][k] + (1.0 - beta_one) * value
        second = beta_two * sc["m2"][k] + (1.0 - beta_two) * value * value
        m1_out[k] = first
        m2_out[k] = second
        step = first / correct_one / (jnp.sqrt(second / correct_two) + adam_eps)
        both = sc["both"]
        both[k, dp, 0] = step.astype(BF16)
        both[k, dp, 1] = value.astype(BF16)
        out = []
        for d in range(1, chips):
            to = lax.rem(chip + d, chips)
            c = remote(both.at[k, dp], both.at[k, dp], sc["s_mix"].at[k], sc["r_mix"].at[k, d - 1], at_chip(to))
            c.start()
            out.append(c)
        c = remote(both.at[k, dp], both.at[k, dp], sc["s_mixf"].at[k], sc["r_mixf"].at[k], partner)
        c.start()
        live["mix", k] = out

    def pass_on(k):
        both = sc["both"]
        out = live["mix", k]
        for d in range(1, chips):
            out[d - 1].wait_recv()
            at = 2 * lax.rem(chip + chips - d, chips) + core
            c = remote(both.at[k, at], both.at[k, at], sc["s_mixf"].at[k], sc["r_mixf"].at[k], partner)
            c.start()

    def back(k):
        taken(sc["both"].at[k, pl.ds(0, chips)], sc["r_mixf"].at[k])
        both, update, row_in = sc["both"], sc["update"], sc["row_in"]
        steps = both[k, :, 0].reshape(rank, cols).astype(F32)
        half = both[k, :, 1].reshape(rank, cols).astype(F32)
        step_norm = jnp.sqrt(jnp.sum(steps * steps, axis=0, keepdims=True))
        grad_norm = jnp.sqrt(jnp.sum(half * half, axis=0, keepdims=True))
        scale = step_norm / (grad_norm + norm_eps)
        sc["mixed"][...] = (steps - scale * half).astype(BF16)
        for ch in range(CB):
            w = sc["weights"][k, :, rows_b(ch)].reshape(chips * step_b, rank)
            value = jnp.dot(w, sc["mixed"][...], preferred_element_type=F32)
            g = sc["grad"][k, :, rows_b(ch)].reshape(chips * step_b, cols).astype(F32)
            value = (value + scale * g).astype(BF16)
            for t in range(chips):
                update[k, t, rows_b(ch)] = value[t * step_b : (t + 1) * step_b]
            for d in range(1, chips):
                to = lax.rem(chip + d, chips)
                c = remote(
                    update.at[k, to, rows_b(ch)], row_in.at[k, chip, rows_b(ch)],
                    sc["s_back"].at[k], sc["r_back"].at[k, ch], at_chip(to),
                )
                c.start()
            row_in[k, chip, rows_b(ch)] = update[k, chip, rows_b(ch)]

    def home(k, ch):
        row_in, plane_in = sc["row_in"], sc["plane_in"][k][ch]
        taken(row_in.at[k, pl.ds(0, chips - 1), rows_b(ch)], sc["r_back"].at[k, ch])
        for dz in range(1, m):
            to = lax.rem(own + dz, m)
            c = remote(
                row_in.at[k, to, rows_b(ch)], plane_in.at[own],
                sc["s_home"].at[k], sc["r_home"].at[k, ch], (dp, to),
            )
            c.start()
        plane_in[own] = row_in[k, own, rows_b(ch)]

    def pick(g, ch):
        q0, q1, last = gather[g]
        for k in range(last + 1):
            if (k, ch) not in live:
                live[k, ch] = True
                taken(sc["plane_in"][k][ch].at[pl.ds(0, m - 1)], sc["r_home"].at[k, ch])
        for q in range(q0, q1):
            value = sc["plane_in"][ranks[q][0]][ch][owner_at[q]]
            for k in ranks[q][1:]:
                here = (rank_at[q] == k).astype(F32)
                value = (
                    value.astype(F32) * (1.0 - here) + sc["plane_in"][k][ch][owner_at[q]].astype(F32) * here
                ).astype(BF16)
            gat[core, yb, xa, q, rows_b(ch)] = value
        block = gat.at[core, yb, xa, pl.ds(q0, q1 - q0), rows_b(ch)]
        out = []
        for d, _, device in peers(ch % 2):
            c = remote(block, block, sc["s_ag1"].at[g, ch, d - 1], sc["r_ag1"].at[g, ch, d - 1], device)
            c.start()
            out.append(c)
        live["ag1", g, ch] = out

    def spread(g, ch):
        q0, q1, _ = gather[g]
        qs = pl.ds(q0, q1 - q0)
        axis = ch % 2
        out = live["ag1", g, ch]
        for c in out:
            c.wait_recv()
        block = gat.at[core, yb, :, qs, rows_b(ch)] if axis == 0 else gat.at[core, :, xa, qs, rows_b(ch)]
        nxt = []
        for d, _, device in peers(1 - axis):
            c = remote(block, block, sc["s_ag2"].at[g, ch, d - 1], sc["r_ag2"].at[g, ch, d - 1], device)
            c.start()
            nxt.append(c)
        c = remote(block, block, sc["s_agp"].at[g], sc["r_agp"].at[g], partner)
        c.start()
        live["ag2", g, ch] = nxt
        sends.extend(out)

    def hand(g, ch):
        q0, q1, _ = gather[g]
        qs = pl.ds(q0, q1 - q0)
        axis = ch % 2
        for i, c in enumerate(live["ag2", g, ch]):
            c.wait_recv()
            d = i + 1
            if axis == 0:
                block = gat.at[core, lax.rem(yb + deep - d, deep), :, qs, rows_b(ch)]
            else:
                block = gat.at[core, :, 1 - xa, qs, rows_b(ch)]
            f = remote(block, block, sc["s_agp"].at[g], sc["r_agp"].at[g], partner)
            f.start()
        sends.extend(live["ag2", g, ch])

    events = []
    for g in range(len(scatter)):
        for ch in range(CH):
            events.append((1.5 + 0.4 * ch if g == 0 else 6.7 + 2.8 * (ch // 2) + 0.1 * ch, first_sum, (g, ch)))
            events.append(((6.3 if g == 0 else 11.1) + 2.8 * (ch // 2) + 0.1 * ch, second_sum, (g, ch)))
            events.append(((10.8 if g == 0 else 15.5) + 1.9 * (ch // 2) + 0.1 * ch, third_sum, (g, ch)))
    middle = [
        (project, (21.0, 27.5, 32.0)), (share, (22.5, 28.8, 33.3)), (adam, (26.5, 33.2, 38.0)),
        (pass_on, (32.5, 39.0, 44.5)), (back, (33.7, 40.2, 45.7)),
    ]
    leave, arrive = (38.0, 44.0, 50.0), (43.5, 49.5, 55.5)
    for k in range(cap):
        for step, times in middle:
            events.append((times[k], step, (k,)))
        for ch in range(CB):
            events.append((leave[k] + 0.7 * ch, home, (k, ch)))
    for g in range(len(gather)):
        base = arrive[gather[g][2]]
        for ch in range(CB):
            events.append((base + 1.3 * ch, pick, (g, ch)))
            events.append((base + 3.2 + 1.3 * ch, spread, (g, ch)))
            events.append((base + 6.5 + 1.3 * ch, hand, (g, ch)))
    for _, step, args in sorted(events, key=lambda e: e[0]):
        step(*args)
    for g, (q0, q1, _) in enumerate(gather):
        taken(gat.at[other, :, :, pl.ds(q0, q1 - q0)], sc["r_agp"].at[g])
    for c in sends:
        c.wait_send()
    sent(grads.at[:, other], sc["s_pair"].at[0])
    sent(sc["slot_out"].at[:, :, pl.ds(1, m - 1)], sc["s_slot"].at[1])

    @pl.when(chip != own)
    def _():
        sent(sc["slot_out"].at[:, :, 0], sc["s_slot"].at[0])

    for k in range(cap):
        sent(sc["share_in"].at[k], sc["s_share"].at[k])
        sent(sc["both"].at[k, pl.ds(0, chips - 1)], sc["s_mix"].at[k])
        sent(sc["both"].at[k, pl.ds(0, chips)], sc["s_mixf"].at[k])
        sent(sc["update"].at[k, pl.ds(0, chips - 1)], sc["s_back"].at[k])
        sent(sc["row_in"].at[k, pl.ds(0, m - 1)], sc["s_home"].at[k])
    for g, (q0, q1, _) in enumerate(gather):
        sent(gat.at[core, :, :, pl.ds(q0, q1 - q0)], sc["s_agp"].at[g])


def place(plan, gat, first, second, out, m1_out, m2_out, sem):
    mats = out.shape[0]
    _, _, pos = plan_scalars(plan, mats)
    copies = []
    for j in range(mats):
        copies.append(pltpu.make_async_copy(gat.at[:, :, :, pos[j]], out.at[j], sem.at[j]))
    copies.append(pltpu.make_async_copy(first, m1_out, sem.at[mats]))
    copies.append(pltpu.make_async_copy(second, m2_out, sem.at[mats + 1]))
    for c in copies:
        c.start()
    for c in copies:
        c.wait()


def local(grads, proj, moment1, moment2, plan):
    n = lax.axis_size("dp")
    m = lax.axis_size("own")
    chips = n // 2
    wide, deep = 2, chips // 2
    mats, own_rows, cols = grads.shape[1:]
    cap, held_rows, rank = proj.shape[1:]
    rank_rows = moment1.shape[2]
    piece = held_rows // chips
    assert chips == m
    g = grads.reshape(mats, 2, chips, piece, cols)
    w = proj.reshape(cap, chips, piece, rank)
    vmem = pl.BlockSpec(memory_space=pltpu.VMEM)
    smem = pl.BlockSpec(memory_space=pltpu.SMEM)
    anywhere = pl.BlockSpec(memory_space=pl.ANY)
    dma = pltpu.SemaphoreType.DMA
    _, scatter, gather = groups_of(mats, m, cap)
    rf, rb = piece // CH, piece // CB
    share_shape = (cap, rank_rows, cols)

    def half(*shape):
        return pltpu.VMEM(shape, BF16)

    def first_axis(ch):
        return (1, deep) if ch % 2 == 0 else (deep - 1, wide)

    sizes = [q1 - q0 for q0, q1, _ in scatter]
    sg, gg = len(scatter), len(gather)
    hops = max(1, deep - 1)
    scratch = dict(
        own_half=[half(mats, chips, rf, cols)] * CH,
        pair_half=[half(mats, chips, rf, cols)] * CH,
        hs=[[half(deep, wide, p, rf, cols)] * CH for p in sizes],
        r1=[[half(*first_axis(ch), p, rf, cols) for ch in range(CH)] for p in sizes],
        s1=[[half(first_axis(ch)[1], p, rf, cols) for ch in range(CH)] for p in sizes],
        r2=[[half(deep - 1 if ch % 2 == 0 else 1, p, rf, cols) for ch in range(CH)] for p in sizes],
        total=[half(mats, rf, cols)] * CH,
        slot_out=half(cap, CH, m, rf, cols),
        grad=half(cap, chips, piece, cols),
        weights=half(cap, chips, piece, rank),
        m1=pltpu.VMEM(share_shape, F32),
        m2=pltpu.VMEM(share_shape, F32),
        part=half(2, cap, chips, rank_rows, cols),
        part_in=half(cap, chips, rank_rows, cols),
        pair_sum=half(cap, chips, rank_rows, cols),
        share_in=half(cap, chips - 1, rank_rows, cols),
        both=half(cap, n, 2, rank_rows, cols),
        mixed=half(rank, cols),
        update=half(cap, chips, piece, cols),
        row_in=half(cap, chips, piece, cols),
        plane_in=[[half(m, rb, cols)] * CB for _ in range(cap)],
        l_own=dma((CH,)), l_rest=dma((3,)),
        s_pair=dma((1,)), r_pair=dma((CH,)),
        s_rs1=dma((sg, CH, hops)), r_rs1=dma((sg, CH, hops)),
        s_rs2=dma((sg, CH, hops)), r_rs2=dma((sg, CH, hops)),
        s_slot=dma((2,)), r_slot=dma((cap, chips)),
        s_part=dma((cap,)), r_part=dma((cap,)),
        s_share=dma((cap,)), r_share=dma((cap,)),
        s_mix=dma((cap,)), r_mix=dma((cap, chips - 1)),
        s_mixf=dma((cap,)), r_mixf=dma((cap,)),
        s_back=dma((cap,)), r_back=dma((cap, CB)),
        s_home=dma((cap,)), r_home=dma((cap, CB)),
        s_ag1=dma((gg, CB, hops)), r_ag1=dma((gg, CB, hops)),
        s_ag2=dma((gg, CB, hops)), r_ag2=dma((gg, CB, hops)),
        s_agp=dma((gg,)), r_agp=dma((gg,)),
    )
    gathered, first, second = pl.pallas_call(
        functools.partial(kernel, n, m),
        out_shape=(
            pltpu.VMEM((2, deep, wide, mats, piece, cols), BF16),
            pltpu.VMEM(share_shape, F32),
            pltpu.VMEM(share_shape, F32),
        ),
        in_specs=[smem] + [anywhere] * 4,
        out_specs=(vmem, vmem, vmem),
        scratch_shapes=[scratch],
        compiler_params=pltpu.CompilerParams(collective_id=0, has_side_effects=True),
    )(plan, g, w, moment1[0], moment2[0])
    stay = functools.partial(pltpu.with_memory_space_constraint, memory_space=pltpu.VMEM)
    update, first, second = pl.pallas_call(
        place,
        out_shape=(
            jax.ShapeDtypeStruct((mats, 2, deep, wide, piece, cols), BF16),
            jax.ShapeDtypeStruct(share_shape, F32),
            jax.ShapeDtypeStruct(share_shape, F32),
        ),
        in_specs=[smem, vmem, vmem, vmem],
        out_specs=(anywhere,) * 3,
        scratch_shapes=[dma((mats + 2,))],
    )(plan, stay(gathered), stay(first), stay(second))
    return (update.reshape(mats, own_rows, cols), first[None], second[None])


def solution(mesh):
    return jax.shard_map(
        local,
        mesh=mesh,
        in_specs=(
            P("dp", None, "own", None),
            P("own", None, "dp", None),
            P("own", None, "dp", None),
            P("own", None, "dp", None),
            P(),
        ),
        out_specs=(P(None, "own", None), P("own", None, "dp", None), P("own", None, "dp", None)),
        check_vma=False,
    )
```
